256 devices in a mesh: freq: 32 (over y, z), tcol: 4 (over x), trow: 2 (over core).
Axes of the slice: x: 4, y: 4, z: 8, core: 2. Of those that a mesh axis runs over, the one named last changes fastest.
Arguments:
- focal_field: bfloat16 [128, 6144, 256], P('freq', ('tcol', 'trow')), may hold values from -6 to 6
- mute_window: int32 [128, 6144], P('freq', ('tcol', 'trow')), may hold values from 64 to 255
- tile_ranks: int32 [32, 16, 16], P('freq', None, ('tcol', 'trow')), may hold values from 32 to 96
- left_factors: bfloat16 [32, 16, 16, 96, 2, 384], P('freq', ('tcol', 'trow')), may hold values from -0.15625 to 0.15625
- right_factors: bfloat16 [32, 16, 16, 96, 2, 384], P('freq', None, ('tcol', 'trow')), may hold values from -0.3125 to 0.3125
Outputs:
- first_pass: bfloat16 [128, 6144, 256], P('freq', ('tcol', 'trow'))
- second_pass: bfloat16 [128, 6144, 256], P('freq', ('tcol', 'trow'))
The draws below stay inside these ranges and needn't reach their ends.
Inputs may be any that keep to these rules, and one draw needn't show every extreme that they name: `mute_window`: samples at times below this index are kept, the others set to zero. Only the first tile_ranks components of a tile's factors enter the operator.
All inputs are finite; a program needn't handle non-finite values.
Results may differ from the reference program's by a relative error of at most 0.013.
Values may be sent and summed in bfloat16 or wider, within the bound.
No kernel may reach another device: no remote copies, remote signals or barrier semaphores. Data moves between devices by JAX's collectives and lax.ppermute only.
A program may use at most 64 MiB of HBM per device.

```python
import math
import jax
import jax.numpy as jnp
from jax import lax

NP = 128
NF = 32
NT = 256
TILE = 384
NTILES = 16
RMAX = 96
RMIN = 32
NS = 6144


def place_ends(drawn, key, smallest, largest):
    dims = drawn.shape
    place = [jax.random.randint(jax.random.fold_in(key, axis), (), 0, dims[axis]) for axis in range(len(dims))]
    drawn = drawn.at[tuple(place)].set(smallest)
    longest = dims.index(max(dims))
    place[longest] = (place[longest] + 1) % dims[longest]
    return drawn.at[tuple(place)].set(largest)


def block_levels(stream_key, dims, split, low, top_value):
    level, own = 1.0, jax.random.fold_in(stream_key, 6)
    for axis_at, shards_of in split:
        steps = jnp.exp(jax.random.uniform(jax.random.fold_in(own, axis_at), (shards_of,), jnp.float32, low / len(split), top_value / len(split)))
        level = level * jnp.repeat(steps, dims[axis_at] // shards_of).reshape([-1 if axis == axis_at else 1 for axis in range(len(dims))])
    return level


def noise(own_key, dims, scale, reach, pieces=(), kind=jnp.bfloat16):
    level = block_levels(own_key, dims, pieces, -0.22, 0.18) if pieces else 1.0
    values = jax.random.normal(own_key, dims, jnp.float32) * scale * level
    return jnp.minimum(jnp.maximum(values, -reach), reach).astype(kind)


def setup_inputs(seed: int = 0) -> dict:
    key_list = jax.random.split(jax.random.key(seed), 6)
    return {
        "focal_field": noise(key_list[0], (NP, NS, NT), 1.0, 6.0, ((0, 32), (1, 8))),
        "mute_window": place_ends(jax.random.randint(key_list[1], (NP, NS), NT // 4, NT), jax.random.fold_in(key_list[1], 1), NT // 4, NT - 1).astype(jnp.int32),
        "tile_ranks": place_ends(jax.random.randint(key_list[2], (NF, NTILES, NTILES), RMIN, RMAX + 1), jax.random.fold_in(key_list[2], 1), RMIN, RMAX).astype(jnp.int32),
        "left_factors": noise(key_list[3], (NF, NTILES, NTILES, RMAX, 2, TILE), (NTILES * RMAX) ** -0.5, 0.15625, ((0, 32), (1, 8))),
        "right_factors": noise(key_list[4], (NF, NTILES, NTILES, RMAX, 2, TILE), TILE ** -0.5, 0.3125, ((0, 32), (2, 8))),
    }


def spectral_table(count_freq, time_len):
    bins = jnp.arange(1, count_freq + 1, dtype=jnp.int32)
    times = jnp.arange(time_len, dtype=jnp.int32)
    turns = bins[:, None] * times[None, :] % time_len
    phase = turns.astype(jnp.float32) * (2.0 * math.pi / time_len)
    return jnp.stack([jnp.cos(phase), -jnp.sin(phase)]).astype(jnp.bfloat16)

def forward(signal, spectral):
    spectrum = jnp.einsum('dft,pst->dfps', spectral.astype(jnp.float32), signal.astype(jnp.float32))
    return (spectrum * (1.0 / math.sqrt(NT))).astype(jnp.bfloat16)

def backward(replies, spectral, keep_time):
    wave_field = jnp.einsum('fdps,dft->pst', replies.astype(jnp.float32), spectral.astype(jnp.float32))
    wave_field = wave_field * (2.0 / math.sqrt(NT))
    return jnp.where(keep_time, wave_field, jnp.zeros_like(wave_field)).astype(jnp.bfloat16)

def apply_one(spec_freq, left_freq, right_freq, rank_freq, conj_sign):
    source_spec = spec_freq.astype(jnp.float32).reshape(2, NP, NTILES, TILE)
    products = jnp.einsum('ijkcl,dpjl->ijkcdp', right_freq.astype(jnp.float32), source_spec)
    real_part = products[:, :, :, 0, 0] + conj_sign * products[:, :, :, 1, 1]
    imag_part = products[:, :, :, 0, 1] - conj_sign * products[:, :, :, 1, 0]
    used_rank = jnp.arange(RMAX, dtype=jnp.int32)[None, None, :] < rank_freq[:, :, None]
    stacked = jnp.stack([real_part, imag_part], axis=3)
    coefficients = jnp.where(used_rank[:, :, :, None, None], stacked, jnp.zeros_like(stacked)).astype(jnp.bfloat16)
    outer_prod = jnp.einsum('ijkcl,ijkdp->cdpil', left_freq.astype(jnp.float32), coefficients.astype(jnp.float32))
    reply_real = outer_prod[0, 0] - conj_sign * outer_prod[1, 1]
    reply_imag = outer_prod[0, 1] + conj_sign * outer_prod[1, 0]
    return jnp.stack([reply_real, reply_imag]).reshape(2, NP, NS).astype(jnp.bfloat16)

def application(signal, spectral, keep_time, tile_ranks, left_factors, right_factors, conj_sign):
    spectrum = forward(signal, spectral)
    by_freq = jnp.moveaxis(spectrum, 1, 0)

    def one_freq(items):
        return apply_one(items[0], items[1], items[2], items[3], conj_sign)
    replies = lax.map(one_freq, (by_freq, left_factors, right_factors, tile_ranks))
    return backward(replies, spectral, keep_time)

def reference(focal_field, mute_window, tile_ranks, left_factors, right_factors):
    spectral = spectral_table(NF, NT)
    keep_time = jnp.arange(NT, dtype=jnp.int32)[None, None, :] < mute_window[:, :, None]
    muted = jnp.where(keep_time, focal_field, jnp.zeros_like(focal_field))
    first_pass = application(muted, spectral, keep_time, tile_ranks, left_factors, right_factors, 1.0)
    second_pass = application(first_pass, spectral, keep_time, tile_ranks, left_factors, right_factors, -1.0)
    return (first_pass, second_pass)
```

```python
import functools
import math

import jax
import jax.numpy as jnp
import numpy as np
from jax import lax
from jax.experimental import pallas as pl
from jax.experimental.pallas import tpu as pltpu
from jax.sharding import PartitionSpec as P

MIB = 1 << 20


def spectral_rows(count_freq, time_len, repeat):
    row = np.arange(count_freq * 2 * repeat)
    bins = row // (2 * repeat) + 1
    part = (row // repeat) % 2
    turns = bins[:, None] * np.arange(time_len)[None, :] % time_len
    phase = turns.astype(np.float32) * np.float32(2.0 * math.pi / time_len)
    table = np.where(part[:, None] == 0, np.cos(phase), -np.sin(phase))
    return jnp.asarray(table.astype(np.float32)).astype(jnp.bfloat16)


def nt_dot(a, b):
    return lax.dot_general(a, b, (((1,), (1,)), ((), ())), preferred_element_type=jnp.float32)


def tn_dot(a, b):
    return lax.dot_general(a, b, (((0,), (0,)), ((), ())), preferred_element_type=jnp.float32)


def swap_parts(x, half):
    rows, cols = x.shape
    grouped = x.reshape(rows // (2 * half), 2 * half, cols)
    return pltpu.roll(grouped, half, axis=1).reshape(rows, cols)


def part_sign(shape, half, sign):
    row = lax.broadcasted_iota(jnp.int32, shape, 0)
    return jnp.where(row % (2 * half) < half, sign, -sign).astype(jnp.float32)


def pick_point(table, point, points):
    row = lax.broadcasted_iota(jnp.int32, table.shape, 0)
    return jnp.where(row % points == point, table, jnp.zeros_like(table))


def to_freq(table, signals, scale):
    points = len(signals)
    total = None
    for point in range(points):
        part = nt_dot(pick_point(table, point, points), signals[point])
        total = part if total is None else total + part
    return (total * scale).astype(jnp.bfloat16)


def to_time(table, replies, window, scale, points):
    flipped = replies.T
    blocks = []
    for point in range(points):
        wave = jnp.dot(
            flipped, pick_point(table, point, points), preferred_element_type=jnp.float32
        ) * scale
        time_at = lax.broadcasted_iota(jnp.int32, wave.shape, 1)
        kept = time_at < window[:, point : point + 1]
        blocks.append(jnp.where(kept, wave, jnp.zeros_like(wave)).astype(jnp.bfloat16))
    return blocks


def stand_window(window):
    wide = window.astype(jnp.float32)
    padded = jnp.concatenate([wide, jnp.zeros((8 - wide.shape[0], wide.shape[1]), jnp.float32)])
    return padded.T.astype(jnp.int32)


def first_kernel(scale, table_ref, field_ref, window_ref, out_ref):
    points = field_ref.shape[0]
    signals = []
    window = stand_window(window_ref[...])
    for point in range(points):
        block = field_ref[point].astype(jnp.float32)
        time_at = lax.broadcasted_iota(jnp.int32, block.shape, 1)
        kept = time_at < window[:, point : point + 1]
        signals.append(jnp.where(kept, block, jnp.zeros_like(block)).astype(jnp.bfloat16))
    out_ref[...] = to_freq(table_ref[...], signals, scale)


def middle_kernel(back_scale, scale, table_ref, reply_ref, window_ref, pass_ref, out_ref):
    points = pass_ref.shape[0]
    table = table_ref[...]
    blocks = to_time(table, reply_ref[...], stand_window(window_ref[...]), back_scale, points)
    for point in range(points):
        pass_ref[point] = blocks[point]
    out_ref[...] = to_freq(table, blocks, scale)


def last_kernel(back_scale, table_ref, reply_ref, window_ref, pass_ref):
    points = pass_ref.shape[0]
    blocks = to_time(table_ref[...], reply_ref[...], stand_window(window_ref[...]), back_scale, points)
    for point in range(points):
        pass_ref[point] = blocks[point]


def right_kernel(rank_ref, factor_ref, out_ref):
    _, all_tiles, col_tiles, rank_cap, parts, tile_len = factor_ref.shape
    block = 16

    def one_tile(number, carry):
        tile, col = number // col_tiles, number % col_tiles
        rank = rank_ref[tile, col]
        for start in range(0, rank_cap, block):
            rows = pl.ds(pl.multiple_of(tile * rank_cap + start, block), block)

            @pl.when(start < rank)
            def _():
                part = factor_ref[0, tile, col, start : start + block]
                part = part.reshape(block, parts * tile_len)
                row = lax.broadcasted_iota(jnp.int32, part.shape, 0) + start
                out_ref[col, rows] = jnp.where(row < rank, part, jnp.zeros_like(part))

            @pl.when(start >= rank)
            def _():
                out_ref[col, rows] = jnp.zeros((block, parts * tile_len), out_ref.dtype)

        return carry

    lax.fori_loop(0, all_tiles * col_tiles, one_tile, 0)


def left_kernel(factor_ref, out_ref):
    _, row_tiles, all_tiles, rank_cap, parts, tile_len = factor_ref.shape

    def one_tile(number, carry):
        tile, col = number // all_tiles, number % all_tiles
        part = factor_ref[0, tile, col].reshape(rank_cap, parts * tile_len)
        out_ref[tile, pl.ds(pl.multiple_of(col * rank_cap, 16), rank_cap)] = part
        return carry

    lax.fori_loop(0, row_tiles * all_tiles, one_tile, 0)


def coef_kernel(sign, half, spec_ref, right_ref, out_ref):
    all_tiles, col_tiles, rank_cap, rows = out_ref.shape
    tile_len = spec_ref.shape[1] // col_tiles
    for col in range(col_tiles):
        block = spec_ref[:, col * tile_len : (col + 1) * tile_len]
        wide = block.astype(jnp.float32)
        other = swap_parts(wide, half) * part_sign(wide.shape, half, sign)
        paired = jnp.concatenate([block, other.astype(jnp.bfloat16)], axis=1)
        coef = nt_dot(right_ref[col], paired).astype(jnp.bfloat16)
        for tile in range(all_tiles):
            out_ref[tile, col] = coef[tile * rank_cap : (tile + 1) * rank_cap]


def reply_kernel(sign, half, coef_ref, left_ref, out_ref):
    sources, row_tiles, depth, rows = coef_ref.shape
    tile_len = out_ref.shape[1] // row_tiles
    for tile in range(row_tiles):
        coef = coef_ref[:, tile].reshape(sources * depth, rows)
        both = tn_dot(coef, left_ref[tile])
        other = both[:, tile_len:]
        other = swap_parts(other, half) * part_sign(other.shape, half, -sign)
        reply = both[:, :tile_len] + other
        out_ref[:, tile * tile_len : (tile + 1) * tile_len] = reply.astype(jnp.bfloat16)


def body(focal_field, mute_window, tile_ranks, left_factors, right_factors):
    points, src_rows, time_len = focal_field.shape
    _, row_tiles, all_tiles, rank_cap, parts_two, tile_len = left_factors.shape
    col_tiles = right_factors.shape[2]
    freqs = lax.axis_size("freq")
    groups = all_tiles // row_tiles
    rows = freqs * 2 * points
    table = spectral_rows(freqs, time_len, points)
    window = mute_window
    scale = 1.0 / math.sqrt(time_len)
    back_scale = 2.0 / math.sqrt(time_len)
    step = 256
    chunks = src_rows // step
    bf16 = jnp.bfloat16

    whole = pl.BlockSpec(memory_space=pltpu.VMEM)
    table_spec = pl.BlockSpec((rows, time_len), lambda s: (0, 0))
    field_spec = pl.BlockSpec((points, step, time_len), lambda s: (0, s, 0))
    window_spec = pl.BlockSpec((points, step), lambda s: (0, s))
    rows_spec = pl.BlockSpec((rows, step), lambda s: (0, s))
    params = pltpu.CompilerParams(vmem_limit_bytes=24 * MIB)
    rows_shape = jax.ShapeDtypeStruct((rows, src_rows), bf16)
    pass_shape = jax.ShapeDtypeStruct(focal_field.shape, bf16)

    smem = pl.BlockSpec(memory_space=pltpu.SMEM)
    with jax.named_scope("prep_right"):
        right = pl.pallas_call(
            right_kernel,
            in_specs=[smem, whole],
            out_specs=whole,
            out_shape=jax.ShapeDtypeStruct(
                (col_tiles, all_tiles * rank_cap, parts_two * tile_len), bf16
            ),
            compiler_params=params,
            name="prep_right",
        )(tile_ranks.reshape(all_tiles, col_tiles), right_factors)
    with jax.named_scope("prep_left"):
        left = pl.pallas_call(
            left_kernel,
            in_specs=[whole],
            out_specs=whole,
            out_shape=jax.ShapeDtypeStruct(
                (row_tiles, all_tiles * rank_cap, parts_two * tile_len), bf16
            ),
            compiler_params=params,
            name="prep_left",
        )(left_factors)

    with jax.named_scope("dft_first"):
        spectrum = pl.pallas_call(
            functools.partial(first_kernel, scale),
            grid=(chunks,),
            in_specs=[table_spec, field_spec, window_spec],
            out_specs=rows_spec,
            out_shape=rows_shape,
            compiler_params=pltpu.CompilerParams(vmem_limit_bytes=58 * MIB),
            name="dft_first",
        )(table, focal_field, window)

    outputs = []
    for number, sign in enumerate((1.0, -1.0)):
        with jax.named_scope(f"to_freq{number}"):
            moved = lax.all_to_all(
                spectrum.reshape(freqs, 2 * points, src_rows), "freq",
                split_axis=0, concat_axis=0, tiled=True,
            ).reshape(rows, src_rows)
        with jax.named_scope(f"coef{number}"):
            coef = pl.pallas_call(
                functools.partial(coef_kernel, sign, points),
                in_specs=[whole, whole],
                out_specs=whole,
                out_shape=jax.ShapeDtypeStruct((all_tiles, col_tiles, rank_cap, rows), bf16),
                compiler_params=params,
                name="coef",
            )(moved, right)
        with jax.named_scope(f"tiles{number}"):
            coef = coef.reshape(groups, row_tiles * col_tiles * rank_cap, rows)
            coef = lax.all_to_all(
                coef, ("tcol", "trow"), split_axis=0, concat_axis=0, tiled=True
            ).reshape(groups, row_tiles, col_tiles * rank_cap, rows)
        with jax.named_scope(f"reply{number}"):
            replies = pl.pallas_call(
                functools.partial(reply_kernel, sign, points),
                in_specs=[whole, whole],
                out_specs=whole,
                out_shape=rows_shape,
                compiler_params=params,
                name="reply",
            )(coef, left)
        with jax.named_scope(f"to_point{number}"):
            replies = lax.all_to_all(
                replies.reshape(freqs, 2 * points, src_rows), "freq",
                split_axis=0, concat_axis=0, tiled=True,
            ).reshape(rows, src_rows)
        if number == 0:
            with jax.named_scope("middle"):
                done, spectrum = pl.pallas_call(
                    functools.partial(middle_kernel, back_scale, scale),
                    grid=(chunks,),
                    in_specs=[table_spec, rows_spec, window_spec],
                    out_specs=(field_spec, rows_spec),
                    out_shape=(pass_shape, rows_shape),
                    compiler_params=params,
                    name="middle",
                )(table, replies, window)
        else:
            with jax.named_scope("last"):
                done = pl.pallas_call(
                    functools.partial(last_kernel, back_scale),
                    grid=(chunks,),
                    in_specs=[table_spec, rows_spec, window_spec],
                    out_specs=field_spec,
                    out_shape=pass_shape,
                    compiler_params=params,
                    name="last",
                )(table, replies, window)
        outputs.append(done)
    return (outputs[0], outputs[1])


def solution(mesh):
    in_specs = (
        P("freq", ("tcol", "trow"), None),
        P("freq", ("tcol", "trow")),
        P("freq", None, ("tcol", "trow")),
        P("freq", ("tcol", "trow"), None, None, None, None),
        P("freq", None, ("tcol", "trow"), None, None, None),
    )
    out_specs = (P("freq", ("tcol", "trow"), None), P("freq", ("tcol", "trow"), None))
    return jax.shard_map(body, mesh=mesh, in_specs=in_specs, out_specs=out_specs, check_vma=False)
```

```python
import functools
import math

import jax
import jax.numpy as jnp
import numpy as np
from jax import lax
from jax.experimental import pallas as pl
from jax.experimental.pallas import tpu as pltpu
from jax.sharding import PartitionSpec as P


MIB = 1 << 20
PARTNERS = ((2, 0), (1, 0), (3, 0), (2, 1), (1, 1), (3, 1), (0, 1), (0, 0))
SPLIT = 5
CALLS = ((0, 2), (2, 5), (5, 8))
EARLY = (7, 6, 0, 1)
LATE = (2, 3, 4, 5)


def spectral_rows(count_freq, time_len, repeat):
    row = np.arange(count_freq * 2 * repeat)
    bins = row // (2 * repeat) + 1
    part = (row // repeat) % 2
    turns = bins[:, None] * np.arange(time_len)[None, :] % time_len
    phase = turns.astype(np.float32) * np.float32(2.0 * math.pi / time_len)
    table = np.where(part[:, None] == 0, np.cos(phase), -np.sin(phase))
    return jnp.asarray(table.astype(np.float32)).astype(jnp.bfloat16)


def nt_dot(a, b):
    return lax.dot_general(a, b, (((1,), (1,)), ((), ())), preferred_element_type=jnp.float32)


def tn_dot(a, b):
    return lax.dot_general(a, b, (((0,), (0,)), ((), ())), preferred_element_type=jnp.float32)


def swap_parts(x, half):
    rows, cols = x.shape
    grouped = x.reshape(rows // (2 * half), 2 * half, cols)
    return pltpu.roll(grouped, half, axis=1).reshape(rows, cols)


def part_sign(shape, half, sign):
    row = lax.broadcasted_iota(jnp.int32, shape, 0)
    return jnp.where(row % (2 * half) < half, sign, -sign).astype(jnp.float32)


def spread_table(table, points, scale):
    row = lax.broadcasted_iota(jnp.int32, table.shape, 0) % points
    scaled = table * jnp.asarray(scale, table.dtype)
    return jnp.concatenate(
        [jnp.where(row == point, scaled, jnp.zeros_like(table)) for point in range(points)], axis=1
    )


def stand_window(window):
    wide = window.astype(jnp.float32)
    padded = jnp.concatenate([wide, jnp.zeros((8 - wide.shape[0], wide.shape[1]), jnp.float32)])
    return padded.T


def mute(block, window):
    rows, length = block.shape
    lanes = 128
    limit = jnp.broadcast_to(window, (rows, lanes)).astype(jnp.bfloat16)
    kept = []
    for start in range(0, length, lanes):
        at = lax.broadcasted_iota(jnp.int32, (rows, lanes), 1) + start
        part = block[:, start : start + lanes]
        kept.append(jnp.where(at.astype(jnp.bfloat16) < limit, part, jnp.zeros_like(part)))
    return jnp.concatenate(kept, axis=1)


def to_freq(table, signals):
    return nt_dot(table, jnp.concatenate(signals, axis=1)).astype(jnp.bfloat16)


def to_time(table, replies, window, points):
    waves = tn_dot(replies, table).astype(jnp.bfloat16)
    length = waves.shape[1] // points
    return [
        mute(waves[:, p * length : (p + 1) * length], window[:, p : p + 1])
        for p in range(points)
    ]


def first_kernel(
    scale, step, table_hbm, window_hbm, field_hbm, out_ref, table_ref, window_ref, field_ref, sems
):
    points, src_rows, _ = field_ref.shape
    small = [
        pltpu.make_async_copy(window_hbm, window_ref, sems.at[points]),
        pltpu.make_async_copy(table_hbm, table_ref, sems.at[points + 1]),
    ]
    copies = [
        pltpu.make_async_copy(field_hbm.at[point], field_ref.at[point], sems.at[point])
        for point in range(points)
    ]
    for copy in small + copies:
        copy.start()
    small[0].wait()
    window = stand_window(window_ref[...])
    small[1].wait()
    table = spread_table(table_ref[...], points, scale)
    for copy in copies:
        copy.wait()
    for start in range(0, src_rows, step):
        signals = [
            mute(
                field_ref[point, start : start + step],
                window[start : start + step, point : point + 1],
            )
            for point in range(points)
        ]
        out_ref[:, start : start + step] = to_freq(table, signals)


def middle_kernel(back_scale, scale, step, table_ref, window_ref, reply_ref, pass_ref, out_ref):
    points, src_rows, _ = pass_ref.shape
    back = spread_table(table_ref[...], points, back_scale)
    table = spread_table(table_ref[...], points, scale)
    window = stand_window(window_ref[...])
    for start in range(0, src_rows, step):
        blocks = to_time(
            back, reply_ref[:, start : start + step], window[start : start + step], points
        )
        for point in range(points):
            pass_ref[point, start : start + step] = blocks[point]
        out_ref[:, start : start + step] = to_freq(table, blocks)


def last_kernel(back_scale, step, table_ref, window_ref, reply_ref, pass_hbm, pass_ref, sems):
    points, src_rows, _ = pass_ref.shape
    table = spread_table(table_ref[...], points, back_scale)
    window = stand_window(window_ref[...])
    copies = []
    for number, start in enumerate(range(0, src_rows, step)):
        part = pl.ds(start, step)
        blocks = to_time(
            table, reply_ref[:, start : start + step], window[start : start + step], points
        )
        for point in range(points):
            pass_ref[point, start : start + step] = blocks[point]
            copies.append(
                pltpu.make_async_copy(
                    pass_ref.at[point, part, :], pass_hbm.at[point, part, :],
                    sems.at[number, point],
                )
            )
            copies[-1].start()
    for copy in copies:
        copy.wait()


def right_kernel(place_ref, rank_ref, factor_ref, early_ref, late_ref):
    _, all_tiles, col_tiles, rank_cap, parts, tile_len = factor_ref.shape
    row_tiles = all_tiles // len(PARTNERS)
    block = 16

    def fill(out_ref, first):
        def one_tile(number, carry):
            at, col = number // col_tiles, number % col_tiles
            slot = at // row_tiles + first
            tile = place_ref[slot] * row_tiles + at % row_tiles
            rank = rank_ref[tile, col]
            for start in range(0, rank_cap, block):
                rows = pl.ds(pl.multiple_of(at * rank_cap + start, block), block)

                @pl.when(start < rank)
                def _():
                    part = factor_ref[0, tile, col, start : start + block]
                    part = part.reshape(block, parts * tile_len)
                    row = lax.broadcasted_iota(jnp.int32, part.shape, 0) + start
                    out_ref[col, rows] = jnp.where(row < rank, part, jnp.zeros_like(part))

                @pl.when(start >= rank)
                def _():
                    out_ref[col, rows] = jnp.zeros((block, parts * tile_len), out_ref.dtype)

            return carry

        lax.fori_loop(0, out_ref.shape[1] // rank_cap * col_tiles, one_tile, 0)

    fill(early_ref, 0)
    fill(late_ref, SPLIT)


def left_kernel(place_ref, factor_ref, out_ref):
    _, row_tiles, all_tiles, rank_cap, parts, tile_len = factor_ref.shape
    col_tiles = all_tiles // len(PARTNERS)

    def one_tile(number, carry):
        tile, at = number // all_tiles, number % all_tiles
        col = place_ref[at // col_tiles] * col_tiles + at % col_tiles
        part = factor_ref[0, tile, col].reshape(rank_cap, parts * tile_len)
        out_ref[tile, pl.ds(pl.multiple_of(at * rank_cap, 16), rank_cap)] = part
        return carry

    lax.fori_loop(0, row_tiles * all_tiles, one_tile, 0)


def coef_kernel(sign, half, first, spec_ref, right_ref, *outs):
    row_tiles, depth, _ = outs[0].shape
    col_tiles = right_ref.shape[0]
    rank_cap = depth // col_tiles
    tile_len = spec_ref.shape[1] // col_tiles
    for col in range(col_tiles):
        block = spec_ref[:, col * tile_len : (col + 1) * tile_len]
        wide = block.astype(jnp.float32)
        other = swap_parts(wide, half) * part_sign(wide.shape, half, sign)
        paired = jnp.concatenate([block, other.astype(jnp.bfloat16)], axis=1)
        span = row_tiles * rank_cap
        factors = right_ref[col, first * span : (first + len(outs)) * span]
        coef = nt_dot(factors, paired).astype(jnp.bfloat16)
        for number in range(len(outs)):
            for tile in range(row_tiles):
                start = (number * row_tiles + tile) * rank_cap
                outs[number][tile, col * rank_cap : (col + 1) * rank_cap] = coef[
                    start : start + rank_cap
                ]


def reply_sum(first, coef_refs, left_ref, tile):
    depth = coef_refs[0].shape[1]
    coef = jnp.concatenate([ref[tile] for ref in coef_refs], axis=0)
    return tn_dot(coef, left_ref[tile, first * depth : (first + len(coef_refs)) * depth])


def early_kernel(*refs):
    *coef_refs, left_ref, out_ref = refs
    for tile in range(out_ref.shape[0]):
        out_ref[tile] = reply_sum(0, coef_refs, left_ref, tile)


def late_kernel(sign, half, *refs):
    *coef_refs, left_ref, sum_ref, out_ref = refs
    tile_len = sum_ref.shape[2] // 2
    for tile in range(sum_ref.shape[0]):
        both = reply_sum(len(EARLY), coef_refs, left_ref, tile) + sum_ref[tile]
        other = both[:, tile_len:]
        other = swap_parts(other, half) * part_sign(other.shape, half, -sign)
        reply = both[:, :tile_len] + other
        out_ref[:, tile * tile_len : (tile + 1) * tile_len] = reply.astype(jnp.bfloat16)


def body(focal_field, mute_window, tile_ranks, left_factors, right_factors):
    points, src_rows, time_len = focal_field.shape
    _, row_tiles, all_tiles, rank_cap, parts_two, tile_len = left_factors.shape
    col_tiles = right_factors.shape[2]
    freqs = lax.axis_size("freq")
    chips, cores = lax.axis_size("tcol"), lax.axis_size("trow")
    rows = freqs * 2 * points
    depth = col_tiles * rank_cap
    table = spectral_rows(freqs, time_len, points)
    scale = 1.0 / math.sqrt(time_len)
    back_scale = 2.0 / math.sqrt(time_len)
    step = 256
    chunks = src_rows // step
    bf16 = jnp.bfloat16
    dma = pltpu.SemaphoreType.DMA

    whole = pl.BlockSpec(memory_space=pltpu.VMEM)
    smem = pl.BlockSpec(memory_space=pltpu.SMEM)
    anywhere = pl.BlockSpec(memory_space=pl.ANY)
    params = pltpu.CompilerParams(vmem_limit_bytes=24 * MIB)
    rows_shape = jax.ShapeDtypeStruct((rows, src_rows), bf16)
    pass_shape = jax.ShapeDtypeStruct(focal_field.shape, bf16)

    def cost(flops, moved):
        return pl.CostEstimate(flops=flops, bytes_accessed=moved, transcendentals=0)

    steps = np.array([s for s, _ in PARTNERS], np.int32)
    other_core = np.array([c for _, c in PARTNERS], np.int32)
    chip, core = lax.axis_index("tcol"), lax.axis_index("trow")
    core_at = jnp.bitwise_xor(core, other_core)
    targets = (chip + steps) % chips * cores + core_at
    order = np.array(EARLY + LATE)
    arriving = jnp.bitwise_xor(core, other_core[order])
    sources = (chip + chips - steps[order]) % chips * cores + arriving
    pairs = []
    for hop, cross in PARTNERS[:-1]:
        pairs.append(
            [
                (x * cores + c, (x + hop) % chips * cores + (c ^ cross))
                for x in range(chips)
                for c in range(cores)
            ]
        )

    factor_size = all_tiles * col_tiles * rank_cap * parts_two * tile_len
    shapes = [
        (col_tiles, count * row_tiles * rank_cap, parts_two * tile_len)
        for count in (SPLIT, len(PARTNERS) - SPLIT)
    ]
    right = pl.pallas_call(
        right_kernel,
        in_specs=[smem, smem, whole],
        out_specs=[whole, whole],
        out_shape=[jax.ShapeDtypeStruct(shape, bf16) for shape in shapes],
        compiler_params=params,
        cost_estimate=cost(0, 6 * factor_size),
        name="prep_right",
    )(targets, tile_ranks.reshape(all_tiles, col_tiles), right_factors)
    spectrum = pl.pallas_call(
        functools.partial(first_kernel, scale, step),
        in_specs=[anywhere, anywhere, anywhere],
        out_specs=whole,
        out_shape=rows_shape,
        scratch_shapes=[
            pltpu.VMEM(table.shape, bf16),
            pltpu.VMEM(mute_window.shape, jnp.int32),
            pltpu.VMEM(focal_field.shape, bf16),
            dma((points + 2,)),
        ],
        compiler_params=pltpu.CompilerParams(vmem_limit_bytes=58 * MIB),
        name="dft_first",
    )(table, mute_window, focal_field)

    def coefficients(sign, moved, begin, end):
        count = end - begin
        factors, first = (right[0], begin) if end <= SPLIT else (right[1], begin - SPLIT)
        return pl.pallas_call(
            functools.partial(coef_kernel, sign, points, first),
            in_specs=[whole, whole],
            out_specs=[whole] * count,
            out_shape=[jax.ShapeDtypeStruct((row_tiles, depth, rows), bf16)] * count,
            compiler_params=params,
            cost_estimate=cost(
                2 * count * row_tiles * depth * parts_two * tile_len * rows,
                count * factor_size // 4,
            ),
            name="coef",
        )(moved, factors)

    def reply_call(kernel, count, out_shape, operands):
        return pl.pallas_call(
            kernel,
            in_specs=[whole] * len(operands),
            out_specs=whole,
            out_shape=out_shape,
            compiler_params=params,
            cost_estimate=cost(
                2 * count * row_tiles * depth * parts_two * tile_len * rows,
                count * factor_size // 4,
            ),
            name="reply",
        )(*operands)

    outputs = []
    outputs = []
    for number, sign in enumerate((1.0, -1.0)):
        moved = lax.all_to_all(
            spectrum.reshape(freqs, 2 * points, src_rows), "freq",
            split_axis=0, concat_axis=0, tiled=True,
        ).reshape(rows, src_rows)
        if number == 0:
            left = pl.pallas_call(
                left_kernel,
                in_specs=[smem, whole],
                out_specs=whole,
                out_shape=jax.ShapeDtypeStruct(
                    (row_tiles, all_tiles * rank_cap, parts_two * tile_len), bf16
                ),
                compiler_params=params,
                cost_estimate=cost(0, 6 * factor_size),
                name="prep_left",
            )(sources, left_factors)
        blocks = []
        for begin, end in CALLS:
            blocks += coefficients(sign, moved, begin, end)
        arrived = []
        for slot, pair in enumerate(pairs):
            arrived.append(lax.ppermute(blocks[slot], ("tcol", "trow"), pair))
        arrived.append(blocks[-1])
        part = reply_call(
            early_kernel, len(EARLY),
            jax.ShapeDtypeStruct((row_tiles, rows, parts_two * tile_len), jnp.float32),
            [arrived[slot] for slot in EARLY] + [left],
        )
        replies = reply_call(
            functools.partial(late_kernel, sign, points), len(LATE), rows_shape,
            [arrived[slot] for slot in LATE] + [left, part],
        )
        replies = lax.all_to_all(
            replies.reshape(freqs, 2 * points, src_rows), "freq",
            split_axis=0, concat_axis=0, tiled=True,
        ).reshape(rows, src_rows)
        if number == 0:
            done, spectrum = pl.pallas_call(
                functools.partial(middle_kernel, back_scale, scale, step),
                in_specs=[whole, whole, whole],
                out_specs=(whole, whole),
                out_shape=(pass_shape, rows_shape),
                compiler_params=params,
                name="middle",
            )(table, mute_window, replies)
        else:
            done = pl.pallas_call(
                functools.partial(last_kernel, back_scale, step),
                in_specs=[whole, whole, whole],
                out_specs=anywhere,
                out_shape=pass_shape,
                scratch_shapes=[pltpu.VMEM(pass_shape.shape, bf16), dma((chunks, points))],
                compiler_params=params,
                name="last",
            )(table, mute_window, replies)
        outputs.append(done)
    return (outputs[0], outputs[1])


def solution(mesh):
    in_specs = (
        P("freq", ("tcol", "trow"), None),
        P("freq", ("tcol", "trow")),
        P("freq", None, ("tcol", "trow")),
        P("freq", ("tcol", "trow"), None, None, None, None),
        P("freq", None, ("tcol", "trow"), None, None, None),
    )
    out_specs = (P("freq", ("tcol", "trow"), None), P("freq", ("tcol", "trow"), None))
    return jax.shard_map(body, mesh=mesh, in_specs=in_specs, out_specs=out_specs, check_vma=False)
```

```python
import functools
import math

import jax
import jax.numpy as jnp
import numpy as np
from jax import lax
from jax.experimental import pallas as pl
from jax.experimental.pallas import tpu as pltpu
from jax.sharding import PartitionSpec as P


MIB = 1 << 20
LANES = 128
PARTNERS = ((2, 0), (2, 1), (1, 0), (3, 0), (1, 1), (3, 1), (0, 1), (0, 0))
SPLIT = 5
CALLS = ((0, 1), (1, 5), (5, 8))
REPLIES = ((7, 6, 0, 1, 2), (3, 4, 5))


def spectral_rows(count_freq, time_len, repeat):
    row = np.arange(count_freq * 2 * repeat)
    bins = row // (2 * repeat) + 1
    part = (row // repeat) % 2
    turns = bins[:, None] * np.arange(time_len)[None, :] % time_len
    phase = turns.astype(np.float32) * np.float32(2.0 * math.pi / time_len)
    table = np.where(part[:, None] == 0, np.cos(phase), -np.sin(phase))
    return jnp.asarray(table.astype(np.float32)).astype(jnp.bfloat16)


def nt_dot(a, b):
    return lax.dot_general(a, b, (((1,), (1,)), ((), ())), preferred_element_type=jnp.float32)


def tn_dot(a, b):
    return lax.dot_general(a, b, (((0,), (0,)), ((), ())), preferred_element_type=jnp.float32)


def swap_parts(x, half):
    rows, cols = x.shape
    grouped = x.reshape(rows // (2 * half), 2 * half, cols)
    return pltpu.roll(grouped, half, axis=1).reshape(rows, cols)


def part_sign(shape, half, sign):
    row = lax.broadcasted_iota(jnp.int32, shape, 0)
    return jnp.where(row % (2 * half) < half, sign, -sign).astype(jnp.float32)


def spread_table(table, points, scale):
    row = lax.broadcasted_iota(jnp.int32, table.shape, 0) % points
    scaled = table * jnp.asarray(scale, table.dtype)
    return jnp.concatenate(
        [jnp.where(row == point, scaled, jnp.zeros_like(table)) for point in range(points)], axis=1
    )


def stand_window(window):
    wide = window.astype(jnp.float32)
    padded = jnp.concatenate([wide, jnp.zeros((8 - wide.shape[0], wide.shape[1]), jnp.float32)])
    return padded.T


def lane_limits(window):
    return jnp.broadcast_to(window, (window.shape[0], LANES)).astype(jnp.bfloat16)


def mute(block, limit):
    kept = []
    for start in range(0, block.shape[1], LANES):
        at = lax.broadcasted_iota(jnp.int32, limit.shape, 1) + start
        part = block[:, start : start + LANES]
        kept.append(jnp.where(at.astype(jnp.bfloat16) < limit, part, jnp.zeros_like(part)))
    return jnp.concatenate(kept, axis=1)


def to_freq(table, signals):
    return nt_dot(table, jnp.concatenate(signals, axis=1)).astype(jnp.bfloat16)


def to_time(table, replies, limits):
    waves = tn_dot(replies, table).astype(jnp.bfloat16)
    points = len(limits)
    length = waves.shape[1] // points
    return [mute(waves[:, p * length : (p + 1) * length], limits[p]) for p in range(points)]


def first_kernel(
    scale, step, table_hbm, window_hbm, field_hbm, out_ref, table_ref, window_ref, field_ref, sems
):
    points, src_rows, _ = field_ref.shape
    chunks = src_rows // step
    small = [
        pltpu.make_async_copy(window_hbm, window_ref, sems.at[points]),
        pltpu.make_async_copy(table_hbm, table_ref, sems.at[points + 1]),
    ]
    copies = [
        pltpu.make_async_copy(field_hbm.at[point], field_ref.at[point], sems.at[point])
        for point in range(points)
    ]
    for copy in small + copies:
        copy.start()
    small[0].wait()
    window = stand_window(window_ref[...])
    limits = [lane_limits(window[:, point : point + 1]) for point in range(points)]
    small[1].wait()
    table = spread_table(table_ref[...], points, scale)
    for copy in copies:
        copy.wait()
    for number in range(chunks):
        part = slice(number * step, (number + 1) * step)
        signals = [mute(field_ref[point, part], limits[point][part]) for point in range(points)]
        out_ref[:, part] = to_freq(table, signals)


def tables_kernel(
    back_scale, scale, table_ref, window_ref, back_ref, turned_ref, forth_ref, limit_ref
):
    points = limit_ref.shape[0]
    table = table_ref[...]
    back = spread_table(table, points, back_scale)
    back_ref[...] = back
    turned_ref[...] = back.astype(jnp.float32).T.astype(jnp.bfloat16)
    forth_ref[...] = spread_table(table, points, scale)
    window = stand_window(window_ref[...])
    for point in range(points):
        limit_ref[point] = lane_limits(window[:, point : point + 1])


def middle_kernel(step, turned_ref, forth_ref, window_ref, reply_ref, pass_ref, out_ref):
    points, length, src_rows = pass_ref.shape
    for start in range(0, src_rows, step):
        part = slice(start, start + step)
        waves = jnp.dot(
            turned_ref[...], reply_ref[:, part], preferred_element_type=jnp.float32
        ).astype(jnp.bfloat16)
        at = lax.broadcasted_iota(jnp.int32, (length, step), 0).astype(jnp.bfloat16)
        kept = []
        for point in range(points):
            limit = window_ref[point : point + 1, part].astype(jnp.float32)
            limit = jnp.broadcast_to(limit, (length, step)).astype(jnp.bfloat16)
            block = waves[point * length : (point + 1) * length]
            kept.append(jnp.where(at < limit, block, jnp.zeros_like(block)))
            pass_ref[point, :, part] = kept[-1]
        signal = jnp.concatenate(kept, axis=0)
        out_ref[:, part] = jnp.dot(
            forth_ref[...], signal, preferred_element_type=jnp.float32
        ).astype(jnp.bfloat16)


def store_kernel(step, turned_ref, pass_hbm, pass_ref, sems):
    points, src_rows, _ = pass_ref.shape
    copies = []
    for point in range(points):
        for start in range(0, src_rows, step):
            block = turned_ref[point, :, start : start + step].astype(jnp.float32)
            pass_ref[point, start : start + step] = block.T.astype(jnp.bfloat16)
        copies.append(
            pltpu.make_async_copy(pass_ref.at[point], pass_hbm.at[point], sems.at[point])
        )
        copies[-1].start()
    for copy in copies:
        copy.wait()


def last_kernel(step, back_ref, limit_ref, reply_ref, pass_hbm, pass_ref, sems):
    points, src_rows, _ = pass_ref.shape
    copies = []
    for number, start in enumerate(range(0, src_rows, step)):
        part = slice(start, start + step)
        limits = [limit_ref[point, part] for point in range(points)]
        blocks = to_time(back_ref[...], reply_ref[:, part], limits)
        for point in range(points):
            pass_ref[point, part] = blocks[point]
            copies.append(
                pltpu.make_async_copy(
                    pass_ref.at[point, pl.ds(start, step), :],
                    pass_hbm.at[point, pl.ds(start, step), :],
                    sems.at[number, point],
                )
            )
            copies[-1].start()
    for copy in copies:
        copy.wait()


def right_kernel(place_ref, rank_ref, factor_ref, early_ref, late_ref):
    _, all_tiles, col_tiles, rank_cap, parts, tile_len = factor_ref.shape
    row_tiles = all_tiles // len(PARTNERS)
    block = 16

    def fill(out_ref, first):
        def one_tile(number, carry):
            at, col = number // col_tiles, number % col_tiles
            slot = at // row_tiles + first
            tile = place_ref[slot] * row_tiles + at % row_tiles
            rank = rank_ref[tile, col]
            for start in range(0, rank_cap, block):
                rows = pl.ds(pl.multiple_of(at * rank_cap + start, block), block)

                @pl.when(start < rank)
                def _():
                    part = factor_ref[0, tile, col, start : start + block]
                    part = part.reshape(block, parts * tile_len)
                    row = lax.broadcasted_iota(jnp.int32, part.shape, 0) + start
                    out_ref[col, rows] = jnp.where(row < rank, part, jnp.zeros_like(part))

                @pl.when(start >= rank)
                def _():
                    out_ref[col, rows] = jnp.zeros((block, parts * tile_len), out_ref.dtype)

            return carry

        lax.fori_loop(0, out_ref.shape[1] // rank_cap * col_tiles, one_tile, 0)

    fill(early_ref, 0)
    fill(late_ref, SPLIT)


def left_kernel(place_ref, factor_ref, out_ref):
    _, row_tiles, all_tiles, rank_cap, parts, tile_len = factor_ref.shape
    col_tiles = all_tiles // len(PARTNERS)

    def one_tile(number, carry):
        tile, at = number // all_tiles, number % all_tiles
        col = place_ref[at // col_tiles] * col_tiles + at % col_tiles
        part = factor_ref[0, tile, col].reshape(rank_cap, parts * tile_len)
        out_ref[tile, pl.ds(pl.multiple_of(at * rank_cap, 16), rank_cap)] = part
        return carry

    lax.fori_loop(0, row_tiles * all_tiles, one_tile, 0)


def coef_kernel(sign, half, first, spec_ref, right_ref, *outs):
    row_tiles, depth, _ = outs[0].shape
    col_tiles = right_ref.shape[0]
    rank_cap = depth // col_tiles
    tile_len = spec_ref.shape[1] // col_tiles
    for col in range(col_tiles):
        block = spec_ref[:, col * tile_len : (col + 1) * tile_len]
        wide = block.astype(jnp.float32)
        other = swap_parts(wide, half) * part_sign(wide.shape, half, sign)
        paired = jnp.concatenate([block, other.astype(jnp.bfloat16)], axis=1)
        span = row_tiles * rank_cap
        factors = right_ref[col, first * span : (first + len(outs)) * span]
        coef = nt_dot(factors, paired).astype(jnp.bfloat16)
        for number in range(len(outs)):
            for tile in range(row_tiles):
                start = (number * row_tiles + tile) * rank_cap
                outs[number][tile, col * rank_cap : (col + 1) * rank_cap] = coef[
                    start : start + rank_cap
                ]


def reply_kernel(sign, half, first, count, starts, ends, *refs):
    coef_refs, left_ref, out_ref = refs[:count], refs[count], refs[-1]
    row_tiles, depth, _ = coef_refs[0].shape
    tile_len = left_ref.shape[2] // 2
    for tile in range(row_tiles):
        coef = jnp.concatenate([ref[tile] for ref in coef_refs], axis=0)
        both = tn_dot(coef, left_ref[tile, first * depth : (first + count) * depth])
        if not starts:
            both = both + refs[count + 1][tile]
        if not ends:
            out_ref[tile] = both
            continue
        other = both[:, tile_len:]
        other = swap_parts(other, half) * part_sign(other.shape, half, -sign)
        reply = both[:, :tile_len] + other
        out_ref[:, tile * tile_len : (tile + 1) * tile_len] = reply.astype(jnp.bfloat16)


def body(focal_field, mute_window, tile_ranks, left_factors, right_factors):
    points, src_rows, time_len = focal_field.shape
    _, row_tiles, all_tiles, rank_cap, parts_two, tile_len = left_factors.shape
    col_tiles = right_factors.shape[2]
    freqs = lax.axis_size("freq")
    chips, cores = lax.axis_size("tcol"), lax.axis_size("trow")
    rows = freqs * 2 * points
    depth = col_tiles * rank_cap
    table = spectral_rows(freqs, time_len, points)
    scale = 1.0 / math.sqrt(time_len)
    back_scale = 2.0 / math.sqrt(time_len)
    step = 256
    chunks = src_rows // step
    bf16 = jnp.bfloat16
    dma = pltpu.SemaphoreType.DMA

    whole = pl.BlockSpec(memory_space=pltpu.VMEM)
    smem = pl.BlockSpec(memory_space=pltpu.SMEM)
    anywhere = pl.BlockSpec(memory_space=pl.ANY)
    params = pltpu.CompilerParams(vmem_limit_bytes=24 * MIB)
    rows_shape = jax.ShapeDtypeStruct((rows, src_rows), bf16)
    pass_shape = jax.ShapeDtypeStruct(focal_field.shape, bf16)
    sums_shape = jax.ShapeDtypeStruct((row_tiles, rows, parts_two * tile_len), jnp.float32)

    def cost(flops, moved):
        return pl.CostEstimate(flops=flops, bytes_accessed=moved, transcendentals=0)

    steps = np.array([s for s, _ in PARTNERS], np.int32)
    other_core = np.array([c for _, c in PARTNERS], np.int32)
    chip, core = lax.axis_index("tcol"), lax.axis_index("trow")
    core_at = jnp.bitwise_xor(core, other_core)
    targets = (chip + steps) % chips * cores + core_at
    order = np.array(sum(REPLIES, ()))
    arriving = jnp.bitwise_xor(core, other_core[order])
    sources = (chip + chips - steps[order]) % chips * cores + arriving
    pairs = []
    for hop, cross in PARTNERS[:-1]:
        pairs.append(
            [
                (x * cores + c, (x + hop) % chips * cores + (c ^ cross))
                for x in range(chips)
                for c in range(cores)
            ]
        )

    factor_size = all_tiles * col_tiles * rank_cap * parts_two * tile_len
    shapes = [
        (col_tiles, count * row_tiles * rank_cap, parts_two * tile_len)
        for count in (SPLIT, len(PARTNERS) - SPLIT)
    ]
    right = pl.pallas_call(
        right_kernel,
        in_specs=[smem, smem, whole],
        out_specs=[whole, whole],
        out_shape=[jax.ShapeDtypeStruct(shape, bf16) for shape in shapes],
        compiler_params=params,
        cost_estimate=cost(0, 6 * factor_size),
        name="prep_right",
    )(targets, tile_ranks.reshape(all_tiles, col_tiles), right_factors)
    spectrum = pl.pallas_call(
        functools.partial(first_kernel, scale, step),
        in_specs=[anywhere, anywhere, anywhere],
        out_specs=whole,
        out_shape=rows_shape,
        scratch_shapes=[
            pltpu.VMEM(table.shape, bf16),
            pltpu.VMEM(mute_window.shape, jnp.int32),
            pltpu.VMEM(focal_field.shape, bf16),
            dma((points + 2,)),
        ],
        compiler_params=pltpu.CompilerParams(vmem_limit_bytes=58 * MIB),
        name="dft_first",
    )(table, mute_window, focal_field)

    def coefficients(sign, moved, begin, end):
        count = end - begin
        factors, first = (right[0], begin) if end <= SPLIT else (right[1], begin - SPLIT)
        return pl.pallas_call(
            functools.partial(coef_kernel, sign, points, first),
            in_specs=[whole, whole],
            out_specs=[whole] * count,
            out_shape=[jax.ShapeDtypeStruct((row_tiles, depth, rows), bf16)] * count,
            compiler_params=params,
            cost_estimate=cost(
                2 * count * row_tiles * depth * parts_two * tile_len * rows,
                count * factor_size // 4,
            ),
            name="coef",
        )(moved, factors)

    def reply_call(sign, arrived, call, total):
        slots = REPLIES[call]
        first = sum(len(group) for group in REPLIES[:call])
        ends = call == len(REPLIES) - 1
        operands = [arrived[slot] for slot in slots] + [left] + ([] if call == 0 else [total])
        return pl.pallas_call(
            functools.partial(
                reply_kernel, sign, points, first, len(slots), call == 0, ends
            ),
            in_specs=[whole] * len(operands),
            out_specs=whole,
            out_shape=rows_shape if ends else sums_shape,
            compiler_params=params,
            cost_estimate=cost(
                2 * len(slots) * row_tiles * depth * parts_two * tile_len * rows,
                len(slots) * factor_size // 4,
            ),
            name="reply",
        )(*operands)

    for number, sign in enumerate((1.0, -1.0)):
        moved = lax.all_to_all(
            spectrum.reshape(freqs, 2 * points, src_rows), "freq",
            split_axis=0, concat_axis=0, tiled=True,
        ).reshape(rows, src_rows)
        if number == 0:
            left = pl.pallas_call(
                left_kernel,
                in_specs=[smem, whole],
                out_specs=whole,
                out_shape=jax.ShapeDtypeStruct(
                    (row_tiles, all_tiles * rank_cap, parts_two * tile_len), bf16
                ),
                compiler_params=params,
                cost_estimate=cost(0, 6 * factor_size),
                name="prep_left",
            )(sources, left_factors)
            tables = pl.pallas_call(
                functools.partial(tables_kernel, back_scale, scale),
                in_specs=[whole, whole],
                out_specs=[whole] * 4,
                out_shape=[
                    jax.ShapeDtypeStruct((rows, points * time_len), bf16),
                    jax.ShapeDtypeStruct((points * time_len, rows), bf16),
                    jax.ShapeDtypeStruct((rows, points * time_len), bf16),
                    jax.ShapeDtypeStruct((points, src_rows, LANES), bf16),
                ],
                compiler_params=params,
                cost_estimate=cost(0, 4 * points * src_rows * LANES),
                name="tables",
            )(table, mute_window)
        if number == 1:
            first = pl.pallas_call(
                functools.partial(store_kernel, step),
                in_specs=[whole],
                out_specs=anywhere,
                out_shape=pass_shape,
                scratch_shapes=[pltpu.VMEM(pass_shape.shape, bf16), dma((points,))],
                compiler_params=params,
                cost_estimate=cost(0, 6 * points * src_rows * time_len),
                name="store",
            )(turned)
        blocks = []
        for begin, end in CALLS:
            blocks += coefficients(sign, moved, begin, end)
        arrived = []
        for slot, pair in enumerate(pairs):
            arrived.append(lax.ppermute(blocks[slot], ("tcol", "trow"), pair))
        arrived.append(blocks[-1])
        replies = None
        for call in range(len(REPLIES)):
            replies = reply_call(sign, arrived, call, replies)
        replies = lax.all_to_all(
            replies.reshape(freqs, 2 * points, src_rows), "freq",
            split_axis=0, concat_axis=0, tiled=True,
        ).reshape(rows, src_rows)
        if number == 0:
            turned, spectrum = pl.pallas_call(
                functools.partial(middle_kernel, step),
                in_specs=[whole] * 4,
                out_specs=(whole, whole),
                out_shape=(jax.ShapeDtypeStruct((points, time_len, src_rows), bf16), rows_shape),
                compiler_params=params,
                name="middle",
            )(tables[1], tables[2], mute_window, replies)
        else:
            second = pl.pallas_call(
                functools.partial(last_kernel, step),
                in_specs=[whole, whole, whole],
                out_specs=anywhere,
                out_shape=pass_shape,
                scratch_shapes=[pltpu.VMEM(pass_shape.shape, bf16), dma((chunks, points))],
                compiler_params=params,
                name="last",
            )(tables[0], tables[3], replies)
    return (first, second)


def solution(mesh):
    in_specs = (
        P("freq", ("tcol", "trow"), None),
        P("freq", ("tcol", "trow")),
        P("freq", None, ("tcol", "trow")),
        P("freq", ("tcol", "trow"), None, None, None, None),
        P("freq", None, ("tcol", "trow"), None, None, None),
    )
    out_specs = (P("freq", ("tcol", "trow"), None), P("freq", ("tcol", "trow"), None))
    return jax.shard_map(body, mesh=mesh, in_specs=in_specs, out_specs=out_specs, check_vma=False)
```
